32 devices in a mesh: seq: 8 (over z, core), tensor: 4 (over y, x).
Axes of the slice: x: 2, y: 2, z: 4, core: 2. Of those that a mesh axis runs over, the one named last changes fastest.
Arguments:
- tokens: bfloat16 [2560, 5120], P('seq'), may hold values from -6 to 6
- gate_weight: bfloat16 [5120, 13824], P('seq', 'tensor'), may hold values from -0.078125 to 0.078125
- up_weight: bfloat16 [5120, 13824], P('seq', 'tensor'), may hold values from -0.078125 to 0.078125
- cotangent: bfloat16 [2560, 13824], P('seq', 'tensor'), may hold values from -24 to 24
- a_mean: float32 [5120, 128], P('seq'), may hold values from -6 to 6
- a_hess: float32 [5120, 128], P('seq'), may hold values from 0.5 to 8
- a_moment: float32 [5120, 128], P('seq'), may hold values from -3 to 3
- a_noise: float32 [5120, 128], P('seq'), may hold values from -6 to 6
- b_mean: float32 [128, 13824], P('seq', 'tensor'), may hold values from -6 to 6
- b_hess: float32 [128, 13824], P('seq', 'tensor'), may hold values from 0.5 to 8
- b_moment: float32 [128, 13824], P('seq', 'tensor'), may hold values from -3 to 3
- b_noise: float32 [128, 13824], P('seq', 'tensor'), may hold values from -6 to 6
Outputs:
- hidden: bfloat16 [2560, 13824], P('seq', 'tensor')
- grad_tokens: bfloat16 [2560, 5120], P(('seq', 'tensor'))
- a_mean_new: float32 [5120, 128], P('seq')
- a_hess_new: float32 [5120, 128], P('seq')
- a_moment_new: float32 [5120, 128], P('seq')
- b_mean_new: float32 [128, 13824], P('seq', 'tensor')
- b_hess_new: float32 [128, 13824], P('seq', 'tensor')
- b_moment_new: float32 [128, 13824], P('seq', 'tensor')
The draws below stay inside these ranges and needn't reach their ends.
All inputs are finite; a program needn't handle non-finite values.
Results may differ from the reference program's by a relative error of at most 0.0095.
Values may be sent and summed in bfloat16 or wider, within the bound.
No kernel may reach another device: no remote copies, remote signals or barrier semaphores. Data moves between devices by JAX's collectives and lax.ppermute only.
A program may use at most 256 MiB of HBM per device.

```python
import math
import jax
import jax.numpy as jnp
from jax import lax

D = 5120
FF_W = 13824
R = 64
TOKENS = 2560
N_TENSOR = 4


def shard_levels(stream_key, dims, shards, smallest, high):
    gain, own = 1.0, jax.random.fold_in(stream_key, 6)
    for axis_at, parts in shards:
        draws = jnp.exp(jax.random.uniform(jax.random.fold_in(own, axis_at), (parts,), jnp.float32, smallest / len(shards), high / len(shards)))
        gain = gain * jnp.repeat(draws, dims[axis_at] // parts).reshape([-1 if axis == axis_at else 1 for axis in range(len(dims))])
    return gain


def bell_draw(key, extent, scale, bound, split=(), held_as=jnp.bfloat16):
    values = jax.random.normal(key, extent, jnp.float32) * scale
    if len(split) > 0:
        values = shard_levels(key, extent, split, -0.22, 0.18) * values
    return jnp.clip(values, min=-bound, max=bound).astype(held_as)


def setup_inputs(seed: int = 0) -> dict:
    streams_of = jax.random.split(jax.random.key(seed), 13)
    return {
        "tokens": bell_draw(streams_of[0], (TOKENS, D), 1.0, 6.0, ((0, 8),)),
        "gate_weight": bell_draw(streams_of[1], (D, FF_W), D ** -0.5, 0.078125, ((0, 8), (1, 4))),
        "up_weight": bell_draw(streams_of[2], (D, FF_W), D ** -0.5, 0.078125, ((0, 8), (1, 4))),
        "cotangent": bell_draw(streams_of[3], (TOKENS, FF_W), 4.0, 24.0, ((0, 8), (1, 4))),
        "a_mean": bell_draw(streams_of[4], (D, 2 * R), 1.0, 6.0, ((0, 8),), jnp.float32),
        "a_hess": jnp.clip(jnp.exp(math.log(8.0) - 2.7725887 * jax.random.uniform(streams_of[5], (D, 2 * R), jnp.float32) ** shard_levels(streams_of[5], (D, 2 * R), ((0, 8),), -0.2, 0.2)), 0.5, 8.0),
        "a_moment": bell_draw(streams_of[6], (D, 2 * R), 0.5, 3.0, ((0, 8),), jnp.float32),
        "a_noise": bell_draw(streams_of[7], (D, 2 * R), 1.0, 6.0, ((0, 8),), jnp.float32),
        "b_mean": bell_draw(streams_of[8], (2 * R, FF_W), 1.0, 6.0, ((0, 8), (1, 4)), jnp.float32),
        "b_hess": jnp.clip(jnp.exp(math.log(8.0) - 2.7725887 * jax.random.uniform(streams_of[9], (2 * R, FF_W), jnp.float32) ** shard_levels(streams_of[9], (2 * R, FF_W), ((0, 8), (1, 4)), -0.2, 0.2)), 0.5, 8.0),
        "b_moment": bell_draw(streams_of[10], (2 * R, FF_W), 0.5, 3.0, ((0, 8), (1, 4)), jnp.float32),
        "b_noise": bell_draw(streams_of[11], (2 * R, FF_W), 1.0, 6.0, ((0, 8), (1, 4)), jnp.float32),
    }


ess = 8.0
decay = 0.001
beta_one = 0.9
beta_two = 0.99
rate = 0.1
debias = 1.0 - 0.9 ** 10

def sample(mean, hess, noise):
    scale = jnp.sqrt(ess * (hess + decay))
    return (mean + noise / scale, scale)

def ivon_update(mean, hess, moment, noise, scale, grad):
    hess_hat = grad * noise * scale
    moment_new = beta_one * moment + (1.0 - beta_one) * grad
    diff = hess - hess_hat
    hess_new = beta_two * hess + (1.0 - beta_two) * hess_hat + 0.5 * (1.0 - beta_two) ** 2 * diff * diff / (hess + decay)
    mean_new = mean - rate * (moment_new / debias + decay * mean) / (hess_new + decay)
    return (mean_new, hess_new, moment_new)

def contract_rows(left, right):
    return lax.dot_general(left, right, (((0,), (0,)), ((), ())), preferred_element_type=jnp.float32)

def reference(tokens, gate_weight, up_weight, cotangent, a_mean, a_hess, a_moment, a_noise, b_mean, b_hess, b_moment, b_noise):
    a_theta, scale_a = sample(a_mean, a_hess, a_noise)
    b_theta, scale_b = sample(b_mean, b_hess, b_noise)
    a_factor = (a_theta / math.sqrt(D)).astype(jnp.bfloat16)
    b_factor = (b_theta / math.sqrt(R)).astype(jnp.bfloat16)
    proj = jnp.dot(tokens, a_factor, preferred_element_type=jnp.float32).astype(jnp.bfloat16)
    gate_pre = jnp.dot(tokens, gate_weight, preferred_element_type=jnp.float32) + jnp.dot(proj[:, :R], b_factor[:R], preferred_element_type=jnp.float32)
    up_pre = jnp.dot(tokens, up_weight, preferred_element_type=jnp.float32) + jnp.dot(proj[:, R:], b_factor[R:], preferred_element_type=jnp.float32)
    sig = jax.nn.sigmoid(gate_pre)
    act = gate_pre * sig
    hidden = (act * up_pre).astype(jnp.bfloat16)
    cot = cotangent.astype(jnp.float32)
    d_gate = (cot * up_pre * sig * (1.0 + gate_pre * (1.0 - sig))).astype(jnp.bfloat16)
    d_up = (cot * act).astype(jnp.bfloat16)
    cols = FF_W // N_TENSOR
    token_total = jnp.zeros((tokens.shape[0], D), jnp.float32)
    rank_total = jnp.zeros((tokens.shape[0], 2 * R), jnp.float32)
    for block in range(N_TENSOR):
        lo = block * cols
        hi = lo + cols
        rank_block = jnp.concatenate([jnp.dot(d_gate[:, lo:hi], b_factor[:R, lo:hi].T, preferred_element_type=jnp.float32), jnp.dot(d_up[:, lo:hi], b_factor[R:, lo:hi].T, preferred_element_type=jnp.float32)], axis=1)
        term = jnp.dot(d_gate[:, lo:hi], gate_weight[:, lo:hi].T, preferred_element_type=jnp.float32)
        term = term + jnp.dot(d_up[:, lo:hi], up_weight[:, lo:hi].T, preferred_element_type=jnp.float32)
        term = term + jnp.dot(rank_block.astype(jnp.bfloat16), a_factor.T, preferred_element_type=jnp.float32)
        token_total = token_total + lax.optimization_barrier(term.astype(jnp.bfloat16)).astype(jnp.float32)
        rank_total = rank_total + rank_block
    grad_tokens = token_total.astype(jnp.bfloat16)
    tokens_all = tokens.shape[0]
    a_grad = jnp.dot(tokens.astype(jnp.float32).T, rank_total, precision=lax.Precision.HIGHEST) / math.sqrt(tokens_all * D)
    b_grad = jnp.concatenate([contract_rows(proj[:, :R], d_gate), contract_rows(proj[:, R:], d_up)], axis=0) / math.sqrt(tokens_all * R)
    a_mean_new, a_hess_new, a_moment_new = ivon_update(a_mean, a_hess, a_moment, a_noise, scale_a, a_grad)
    b_mean_new, b_hess_new, b_moment_new = ivon_update(b_mean, b_hess, b_moment, b_noise, scale_b, b_grad)
    return (hidden, grad_tokens, a_mean_new, a_hess_new, a_moment_new, b_mean_new, b_hess_new, b_moment_new)
```

```python
import functools
import math

import jax
import jax.numpy as jnp
from jax import lax
from jax.experimental import pallas as pl
from jax.experimental.pallas import tpu as pltpu
from jax.sharding import PartitionSpec as P


R = 64
LANE = 128


ess = 8.0
decay = 0.001
beta_one = 0.9
beta_two = 0.99
rate = 0.1
debias = 1.0 - 0.9**10


def sample(mean, hess, noise):
    scale = jnp.sqrt(ess * (hess + decay))
    return (mean + noise / scale, scale)


def ivon_update(mean, hess, moment, noise, scale, grad):
    hess_hat = grad * noise * scale
    moment_new = beta_one * moment + (1.0 - beta_one) * grad
    diff = hess - hess_hat
    hess_new = (
        beta_two * hess
        + (1.0 - beta_two) * hess_hat
        + 0.5 * (1.0 - beta_two) ** 2 * diff * diff / (hess + decay)
    )
    mean_new = mean - rate * (moment_new / debias + decay * mean) / (hess_new + decay)
    return (mean_new, hess_new, moment_new)


def contract_rows(left, right):
    return lax.dot_general(
        left, right, (((0,), (0,)), ((), ())), preferred_element_type=jnp.float32
    )


def contract_lanes(left, right):
    return lax.dot_general(
        left, right, (((1,), (1,)), ((), ())), preferred_element_type=jnp.float32
    )


def gathered_plan(
    tokens,
    gate_weight,
    up_weight,
    cotangent,
    a_mean,
    a_hess,
    a_moment,
    a_noise,
    b_mean,
    b_hess,
    b_moment,
    b_noise,
):
    seq_count = lax.axis_size("seq")
    d_model = gate_weight.shape[0] * seq_count
    tokens_all = tokens.shape[0] * seq_count
    a_theta, scale_a = sample(a_mean, a_hess, a_noise)
    b_theta, scale_b = sample(b_mean, b_hess, b_noise)
    a_piece = (a_theta / math.sqrt(d_model)).astype(jnp.bfloat16)
    b_piece = (b_theta / math.sqrt(R)).astype(jnp.bfloat16)
    a_factor = lax.all_gather(a_piece, "seq", axis=0, tiled=True)
    b_factor = lax.all_gather(b_piece, "seq", axis=0, tiled=True)
    proj = jnp.dot(tokens, a_factor, preferred_element_type=jnp.float32).astype(jnp.bfloat16)
    gate_full = lax.all_gather(gate_weight, "seq", axis=0, tiled=True)
    up_full = lax.all_gather(up_weight, "seq", axis=0, tiled=True)
    gate_base = jnp.dot(tokens, gate_full, preferred_element_type=jnp.float32)
    up_base = jnp.dot(tokens, up_full, preferred_element_type=jnp.float32)
    gate_pre = gate_base + jnp.dot(proj[:, :R], b_factor[:R], preferred_element_type=jnp.float32)
    up_pre = up_base + jnp.dot(proj[:, R:], b_factor[R:], preferred_element_type=jnp.float32)
    sig = jax.nn.sigmoid(gate_pre)
    act = gate_pre * sig
    hidden = (act * up_pre).astype(jnp.bfloat16)
    cot = cotangent.astype(jnp.float32)
    d_gate = (cot * up_pre * sig * (1.0 + gate_pre * (1.0 - sig))).astype(jnp.bfloat16)
    d_up = (cot * act).astype(jnp.bfloat16)
    rank_part = jnp.concatenate(
        [
            jnp.dot(d_gate, b_factor[:R].T, preferred_element_type=jnp.float32),
            jnp.dot(d_up, b_factor[R:].T, preferred_element_type=jnp.float32),
        ],
        axis=1,
    )
    back = jnp.dot(d_gate, gate_full.T, preferred_element_type=jnp.float32)
    back = back + jnp.dot(d_up, up_full.T, preferred_element_type=jnp.float32)
    term = back + jnp.dot(
        rank_part.astype(jnp.bfloat16), a_factor.T, preferred_element_type=jnp.float32
    )
    grad_tokens = lax.psum_scatter(
        term.astype(jnp.bfloat16), "tensor", scatter_dimension=0, tiled=True
    )
    b_part = jnp.concatenate(
        [contract_rows(proj[:, :R], d_gate), contract_rows(proj[:, R:], d_up)], axis=0
    ) / math.sqrt(tokens_all * R)
    rank_high = rank_part.astype(jnp.bfloat16)
    rank_low = (rank_part - rank_high.astype(jnp.float32)).astype(jnp.bfloat16)
    a_part = (contract_rows(tokens, rank_high) + contract_rows(tokens, rank_low)) / math.sqrt(
        tokens_all * d_model
    )
    a_seq = lax.psum_scatter(
        a_part.astype(jnp.bfloat16), "seq", scatter_dimension=0, tiled=True
    ).astype(jnp.float32)
    b_grad = lax.psum_scatter(
        b_part.astype(jnp.bfloat16), "seq", scatter_dimension=0, tiled=True
    ).astype(jnp.float32)
    a_grad = lax.psum(a_seq.astype(jnp.bfloat16), "tensor").astype(jnp.float32)
    a_new = ivon_update(a_mean, a_hess, a_moment, a_noise, scale_a, a_grad)
    b_new = ivon_update(b_mean, b_hess, b_moment, b_noise, scale_b, b_grad)
    return (hidden, grad_tokens, *a_new, *b_new)


def split_rank(value):
    row = lax.broadcasted_iota(jnp.int32, value.shape, 0)
    zero = jnp.zeros_like(value)
    return jnp.concatenate(
        [jnp.where(row < R, value, zero), jnp.where(row >= R, value, zero)], axis=1
    )


def fwd_kernel(zs, cnt, chunk, s_ref, tok_ref, a_ref, b_ref, *refs):
    cot_refs, refs = refs[:zs], refs[zs:]
    w_refs, refs = refs[: 2 * zs], refs[2 * zs :]
    hid_refs, refs = refs[:zs], refs[zs:]
    dg_ref, du_ref, bmat_ref, proj_ref, wcat_s, cot_s, hid_s = refs
    n = pl.program_id(0)
    z, core, col0 = s_ref[0], s_ref[1], s_ref[2]
    tiles = pl.num_programs(0)
    half = a_ref.shape[2]
    part = b_ref.shape[2]
    step = chunk // cnt
    m_all = tok_ref.shape[1] * cnt
    rows = m_all // zs

    def tok(q, m, lanes):
        return tok_ref[q, m // cnt : m // cnt + step, :, lanes].reshape(chunk, -1)

    @pl.when(n == 0)
    def _():
        for m in range(0, m_all, chunk):
            p = jnp.zeros((chunk, 2 * R), jnp.float32)
            for q in range(zs):
                for c in range(2):
                    p += jnp.dot(
                        tok(q, m, slice(c * half, (c + 1) * half)),
                        a_ref[jnp.bitwise_xor(core, c), jnp.bitwise_xor(z, q)],
                        preferred_element_type=jnp.float32,
                    )
            proj_ref[m : m + chunk, :] = p.astype(jnp.bfloat16)

    for k in range(zs):
        q = jnp.bitwise_xor(z, k)
        for side in range(2):
            c = jnp.bitwise_xor(core, side)
            at = pl.ds(pl.multiple_of(c * half, LANE), half)
            w = w_refs[side * zs + k]
            wcat_s[q, at, :LANE] = w[0]
            wcat_s[q, at, LANE:] = w[1]
            at = pl.ds(pl.multiple_of((2 * q + c) * part, part), part)
            bmat_ref[at, :] = b_ref[side, k]
        cot_s[pl.ds(pl.multiple_of(q * rows, 16), rows), :] = cot_refs[k][...]
    keep = col0 + n >= z * tiles
    bb = split_rank(bmat_ref[...])
    for m in range(0, m_all, chunk):
        at = slice(m, m + chunk)
        acc = jnp.dot(proj_ref[at, :], bb, preferred_element_type=jnp.float32)
        for q in range(zs):
            acc += jnp.dot(tok(q, m, slice(None)), wcat_s[q], preferred_element_type=jnp.float32)
        g, u = acc[:, :LANE], acc[:, LANE:]
        sig = jax.nn.sigmoid(g)
        act = g * sig
        hid_s[at, :] = (act * u).astype(jnp.bfloat16)
        cot = cot_s[at, :].astype(jnp.float32)
        dg = cot * u * sig * (1.0 + g * (1.0 - sig))
        dg_ref[at, :] = jnp.where(keep, dg, 0.0).astype(jnp.bfloat16)
        du_ref[at, :] = jnp.where(keep, cot * act, 0.0).astype(jnp.bfloat16)
    for k in range(zs):
        q = jnp.bitwise_xor(z, k)
        hid_refs[k][...] = hid_s[pl.ds(pl.multiple_of(q * rows, 16), rows), :]


def bwd_kernel(zs, ts, cnt, s_ref, dg_ref, du_ref, bmat_ref, a_ref, *refs):
    w_refs, (out_ref, rank_ref, d_s) = refs[: 2 * zs], refs[2 * zs :]
    i = pl.program_id(0)
    z, core = s_ref[0], s_ref[1]
    wide = dg_ref.shape[1]

    @pl.when(i == 0)
    def _():
        d_s[:, :wide] = dg_ref[...]
        d_s[:, wide : 2 * wide] = du_ref[...]
        rank = contract_lanes(d_s[:, : 2 * wide], split_rank(bmat_ref[...]))
        rank_ref[...] = rank
        d_s[:, 2 * wide :] = rank.astype(jnp.bfloat16)

    for k in range(zs):
        q = jnp.bitwise_xor(z, k)
        w = []
        for side in range(2):
            ref = w_refs[side * zs + k]
            w.append(jnp.concatenate([ref[0], ref[1], a_ref[side, k]], axis=1))
        w = jnp.concatenate(w, axis=0)
        acc = contract_lanes(d_s[...], w).astype(jnp.bfloat16)
        for side in range(2):
            blk = 2 * q + jnp.bitwise_xor(core, side)
            part = acc[:, side * LANE : (side + 1) * LANE]
            for zz in range(zs):
                for t in range(ts):
                    m = (zz * ts + t) * cnt
                    out_ref[t, zz, blk] = part[m : m + cnt, :]


def place_kernel(zs, ts, own, sizes, wide, limit, s_ref, *refs):
    out_ref = refs[-1]
    for k in range(zs):
        at = jnp.minimum(jnp.bitwise_xor(s_ref[0], k) * wide, limit)
        at = pl.ds(pl.multiple_of(at, LANE), wide)
        for j, (off, cnt) in enumerate(sizes):
            for t in range(ts):
                out_ref[t * own + off : t * own + off + cnt, at] = refs[j * zs + k][
                    t * cnt : (t + 1) * cnt, :
                ]


def whole(shape):
    return pl.BlockSpec(shape, lambda i, s: (0,) * len(shape), pipeline_mode=pl.Buffered(1))


def forward(scalars, tok, a_all, b_all, cots, weights, off, cnt):
    zs, groups, _, quarter = tok.shape
    m_all = groups * cnt
    rows, wide = cots[0].shape
    half = weights[0].shape[1]
    chunk = m_all // max(1, m_all // 256)
    while chunk % cnt or m_all % chunk:
        chunk += 16
    bf = jnp.bfloat16
    return pl.pallas_call(
        functools.partial(fwd_kernel, zs, cnt, chunk),
        grid_spec=pltpu.PrefetchScalarGridSpec(
            num_scalar_prefetch=1,
            grid=(wide // LANE,),
            in_specs=[
                pl.BlockSpec(
                    (zs, groups, cnt, quarter),
                    lambda i, s: (0, 0, off // cnt, 0),
                    pipeline_mode=pl.Buffered(1),
                ),
                whole(a_all.shape),
                pl.BlockSpec((*b_all.shape[:3], LANE), lambda i, s: (0, 0, 0, i)),
            ]
            + [pl.BlockSpec((rows, LANE), lambda i, s: (0, i))] * zs
            + [pl.BlockSpec((2, half, LANE), lambda i, s: (0, 0, i))] * (2 * zs),
            out_specs=[pl.BlockSpec((rows, LANE), lambda i, s: (0, i))] * zs
            + [pl.BlockSpec((m_all, LANE), lambda i, s: (0, i))] * 2
            + [pl.BlockSpec((2 * R, LANE), lambda i, s: (0, i))]
            + [pl.BlockSpec((m_all, 2 * R), lambda i, s: (0, 0))],
            scratch_shapes=[
                pltpu.VMEM((zs, 2 * half, 2 * LANE), bf),
                pltpu.VMEM((m_all, LANE), bf),
                pltpu.VMEM((m_all, LANE), bf),
            ],
        ),
        out_shape=[jax.ShapeDtypeStruct((rows, wide), bf)] * zs
        + [jax.ShapeDtypeStruct((m_all, wide), bf)] * 2
        + [jax.ShapeDtypeStruct((2 * R, wide), bf)]
        + [jax.ShapeDtypeStruct((m_all, 2 * R), bf)],
        compiler_params=pltpu.CompilerParams(vmem_limit_bytes=44 << 20),
        cost_estimate=pl.CostEstimate(
            flops=2 * m_all * 2 * wide * (2 * zs * half),
            bytes_accessed=4 * zs * half * wide * 2 + m_all * (zs * quarter + 4 * wide) * 2,
            transcendentals=m_all * wide,
        ),
        name="fwd_columns",
    )(scalars, tok, a_all, b_all, *cots, *weights)


def backward(scalars, d_gate, d_up, bmat, a_all, weights, ts, cnt):
    zs = len(weights) // 2
    m_all, wide = d_gate.shape
    half = weights[0].shape[1]
    bf = jnp.bfloat16
    return pl.pallas_call(
        functools.partial(bwd_kernel, zs, ts, cnt),
        grid_spec=pltpu.PrefetchScalarGridSpec(
            num_scalar_prefetch=1,
            grid=(half // LANE,),
            in_specs=[whole(d_gate.shape), whole(d_up.shape), whole(bmat.shape)]
            + [pl.BlockSpec((2, zs, LANE, 2 * R), lambda i, s: (0, 0, i, 0))]
            + [pl.BlockSpec((2, LANE, wide), lambda i, s: (0, i, 0))] * (2 * zs),
            out_specs=[
                pl.BlockSpec((ts, zs, 2 * zs, cnt, LANE), lambda i, s: (0, 0, 0, 0, i)),
                pl.BlockSpec((m_all, 2 * R), lambda i, s: (0, 0)),
            ],
            scratch_shapes=[pltpu.VMEM((m_all, 2 * wide + 2 * R), bf)],
        ),
        out_shape=[
            jax.ShapeDtypeStruct((ts, zs, 2 * zs, cnt, half), bf),
            jax.ShapeDtypeStruct((m_all, 2 * R), jnp.float32),
        ],
        compiler_params=pltpu.CompilerParams(vmem_limit_bytes=44 << 20),
        cost_estimate=pl.CostEstimate(
            flops=2 * m_all * 2 * wide * (2 * zs * half),
            bytes_accessed=4 * zs * half * wide * 2 + m_all * (2 * zs * half + 2 * wide) * 2,
            transcendentals=0,
        ),
        name="bwd_columns",
    )(scalars, d_gate, d_up, bmat, a_all, *weights)


def place(scalars, pieces, zs, ts, own, sizes, cols):
    wide = pieces[0].shape[1]
    return pl.pallas_call(
        functools.partial(place_kernel, zs, ts, own, sizes, wide, cols - wide),
        grid_spec=pltpu.PrefetchScalarGridSpec(
            num_scalar_prefetch=1,
            grid=(1,),
            in_specs=[whole(piece.shape) for piece in pieces],
            out_specs=whole((ts * own, cols)),
        ),
        out_shape=jax.ShapeDtypeStruct((ts * own, cols), jnp.bfloat16),
        compiler_params=pltpu.CompilerParams(vmem_limit_bytes=16 << 20),
        cost_estimate=pl.CostEstimate(
            flops=0, bytes_accessed=4 * ts * own * cols, transcendentals=0
        ),
        name="place_hidden",
    )(scalars, *pieces)


def after(value, *earlier):
    return lax.optimization_barrier((value, *earlier))[0]


def chunk_sizes(own):
    sizes, off = [], 0
    size = max(16, own * 2 // 5 // 16 * 16)
    while off < own:
        cnt = min(size, own - off)
        while off % cnt:
            cnt -= 16
        sizes.append((off, cnt))
        off += cnt
    return tuple(sizes)


def split_plan(
    tokens,
    gate_weight,
    up_weight,
    cotangent,
    a_mean,
    a_hess,
    a_moment,
    a_noise,
    b_mean,
    b_hess,
    b_moment,
    b_noise,
):
    seq_count = lax.axis_size("seq")
    ts = lax.axis_size("tensor")
    zs = seq_count // 2
    half, cols = gate_weight.shape
    d_model = half * seq_count
    rows = tokens.shape[0]
    tokens_all = rows * seq_count
    wide = -(-cols // (zs * LANE)) * LANE
    own = rows // ts
    part = 2 * R // seq_count
    seq = lax.axis_index("seq")
    z, core = seq // 2, seq % 2
    tensor = lax.axis_index("tensor")
    cores = [[2 * j + c for j in range(zs)] for c in range(2)]
    bf = jnp.bfloat16

    def start_of(chip):
        return jnp.minimum(chip * wide, cols - wide)

    def columns(value, k):
        at = start_of(jnp.bitwise_xor(z, k))
        return lax.dynamic_slice_in_dim(value, at, wide, value.ndim - 1)

    def over_z(value, k):
        if k == 0:
            return value
        return lax.ppermute(value, "seq", [(s, s ^ (2 * k)) for s in range(seq_count)])

    def over_core(value):
        return lax.ppermute(value, "seq", [(s, s ^ 1) for s in range(seq_count)])

    scalars = jnp.stack([z, core, start_of(z) // LANE]).astype(jnp.int32)

    a_theta, scale_a = sample(a_mean, a_hess, a_noise)
    b_theta, scale_b = sample(b_mean, b_hess, b_noise)
    a_piece = (a_theta / math.sqrt(d_model)).astype(bf)
    b_piece = (b_theta / math.sqrt(R)).astype(bf)
    a_mine = jnp.stack([over_z(a_piece, k) for k in range(zs)])
    b_mine = jnp.stack([over_z(columns(b_piece, k), k) for k in range(zs)])
    a_all = jnp.stack([a_mine, over_core(a_mine)])
    b_all = jnp.stack([b_mine, over_core(b_mine)])

    pieces = [jnp.stack([columns(gate_weight, k), columns(up_weight, k)]) for k in range(zs)]
    mine = [None] * zs
    mine[0] = pieces[0]
    for k in range(zs - 1, 0, -1):
        mine[k] = over_z(pieces[k], k)
    weights = mine + [over_core(piece) for piece in mine]

    quarter = d_model // ts
    tok = lax.dynamic_slice_in_dim(tokens, tensor * quarter, quarter, 1)
    tok = after(tok, *pieces)
    tok = lax.all_gather(tok, "seq", axis=0, axis_index_groups=cores, tiled=True)
    tok = lax.all_gather(tok, "tensor", axis=0, tiled=False)

    sizes = chunk_sizes(own)
    cots, gate = [], mine[zs - 1]
    for off, cnt in sizes:
        cot = cotangent.reshape(ts, own, cols)[:, off : off + cnt].reshape(ts * cnt, cols)
        cots.append(
            [over_z(after(columns(cot, k), gate) if k else columns(cot, k), k) for k in range(zs)]
        )
        gate = mine[zs - 1], mine[zs - 2]
    tok = tok.reshape(zs, zs * ts, own, quarter)

    hidden, grads, ranks = [], [], []
    b_part = jnp.zeros((2 * R, wide), jnp.float32)
    for (off, cnt), cot in zip(sizes, cots):
        *hid, d_gate, d_up, bmat, proj = forward(scalars, tok, a_all, b_all, cot, weights, off, cnt)
        hidden += [over_z(hid[k], k) for k in range(zs)]
        term, rank = backward(scalars, d_gate, d_up, bmat, a_all, weights, ts, cnt)
        ranks.append(rank.reshape(zs * ts, cnt, 2 * R))
        b_part = b_part + jnp.concatenate(
            [contract_rows(proj[:, :R], d_gate), contract_rows(proj[:, R:], d_up)], axis=0
        )
        term = lax.psum_scatter(
            term.reshape(-1, half), "tensor", scatter_dimension=0, tiled=True
        ).reshape(term.shape[1:])
        total = jnp.zeros(term.shape[1:], jnp.float32)
        for k in range(zs):
            piece = lax.dynamic_index_in_dim(term, jnp.bitwise_xor(z, k), 0, keepdims=False)
            total = total + over_z(piece, k).astype(jnp.float32)
        grads.append(total.astype(bf))

    hidden = place(scalars, hidden, zs, ts, own, sizes, cols)
    grad_tokens = jnp.concatenate(grads, axis=1).transpose(1, 0, 2).reshape(own, d_model)

    rank = jnp.concatenate(ranks, axis=1).reshape(zs * rows, 2 * R)
    rank_high = rank.astype(bf)
    rank_low = (rank - rank_high.astype(jnp.float32)).astype(bf)
    both = jnp.concatenate([rank_high, rank_low], axis=1)
    a_part = jnp.einsum(
        "qmd,mr->qdr",
        tok.reshape(zs, zs * rows, quarter),
        both,
        preferred_element_type=jnp.float32,
    )
    a_part = (a_part[..., : 2 * R] + a_part[..., 2 * R :]) / math.sqrt(tokens_all * d_model)
    a_part = a_part.reshape(zs, 2, half, 2 * R)
    a_keep = lax.dynamic_index_in_dim(a_part, core, 1, keepdims=False)
    a_give = lax.dynamic_index_in_dim(a_part, 1 - core, 1, keepdims=False)
    a_part = (a_keep + over_core(a_give.astype(bf)).astype(jnp.float32)).astype(bf)
    a_seq = jnp.zeros((half, 2 * R), jnp.float32)
    for k in range(zs):
        piece = lax.dynamic_index_in_dim(a_part, jnp.bitwise_xor(z, k), 0, keepdims=False)
        a_seq = a_seq + over_z(piece, k).astype(jnp.float32)
    a_seq = a_seq.astype(bf)
    a_grad = a_seq.astype(jnp.float32)
    for k in range(1, ts):
        a_grad = a_grad + lax.ppermute(
            a_seq, "tensor", [(t, t ^ k) for t in range(ts)]
        ).astype(jnp.float32)

    b_part = (b_part / math.sqrt(tokens_all * R)).astype(bf)
    b_parts = lax.all_to_all(
        b_part.reshape(seq_count, part, wide), "seq", 0, 0, tiled=True
    ).astype(jnp.float32)
    b_parts = b_parts.reshape(zs, 2, part, wide).sum(1)
    b_grad = jnp.concatenate(
        [b_parts[j] for j in range(zs - 1)]
        + [b_parts[zs - 1][:, wide - (cols - (zs - 1) * wide) :]],
        axis=1,
    )

    a_new = ivon_update(a_mean, a_hess, a_moment, a_noise, scale_a, a_grad)
    b_new = ivon_update(b_mean, b_hess, b_moment, b_noise, scale_b, b_grad)
    return (hidden, grad_tokens, *a_new, *b_new)


def on_device(tokens, gate_weight, *rest):
    seq_count, ts = lax.axis_size("seq"), lax.axis_size("tensor")
    zs = seq_count // 2
    half, cols = gate_weight.shape
    rows = tokens.shape[0]
    wide = -(-cols // (zs * LANE)) * LANE
    fits = (
        seq_count == 2 * ts
        and ts & (ts - 1) == 0
        and half % LANE == 0
        and cols % LANE == 0
        and (zs - 1) * wide < cols
        and rows % (16 * ts) == 0
        and 2 * R == 16 * seq_count
        and rows * zs * half * seq_count * 2 <= 16 << 20
    )
    plan = split_plan if fits else gathered_plan
    return plan(tokens, gate_weight, *rest)


def solution(mesh):
    row, both = P("seq", None), P("seq", "tensor")
    in_specs = (row, both, both, both, row, row, row, row, both, both, both, both)
    out_specs = (both, P(("seq", "tensor"), None), row, row, row, both, both, both)
    return jax.shard_map(
        on_device, mesh=mesh, in_specs=in_specs, out_specs=out_specs, check_vma=False
    )
```

```python
import functools
import math

import jax
import jax.numpy as jnp
from jax import lax
from jax.experimental import pallas as pl
from jax.experimental.pallas import tpu as pltpu
from jax.sharding import PartitionSpec as P


R = 64
LANE = 128


ess = 8.0
decay = 0.001
beta_one = 0.9
beta_two = 0.99
rate = 0.1
debias = 1.0 - 0.9**10


def sample(mean, hess, noise):
    scale = jnp.sqrt(ess * (hess + decay))
    return (mean + noise / scale, scale)


def ivon_update(mean, hess, moment, noise, scale, grad):
    hess_hat = grad * noise * scale
    moment_new = beta_one * moment + (1.0 - beta_one) * grad
    diff = hess - hess_hat
    hess_new = (
        beta_two * hess
        + (1.0 - beta_two) * hess_hat
        + 0.5 * (1.0 - beta_two) ** 2 * diff * diff / (hess + decay)
    )
    mean_new = mean - rate * (moment_new / debias + decay * mean) / (hess_new + decay)
    return (mean_new, hess_new, moment_new)


def contract_rows(left, right):
    return lax.dot_general(
        left, right, (((0,), (0,)), ((), ())), preferred_element_type=jnp.float32
    )


def contract_lanes(left, right):
    return lax.dot_general(
        left, right, (((1,), (1,)), ((), ())), preferred_element_type=jnp.float32
    )


def gathered_plan(
    tokens,
    gate_weight,
    up_weight,
    cotangent,
    a_mean,
    a_hess,
    a_moment,
    a_noise,
    b_mean,
    b_hess,
    b_moment,
    b_noise,
):
    seq_count = lax.axis_size("seq")
    d_model = gate_weight.shape[0] * seq_count
    tokens_all = tokens.shape[0] * seq_count
    a_theta, scale_a = sample(a_mean, a_hess, a_noise)
    b_theta, scale_b = sample(b_mean, b_hess, b_noise)
    a_piece = (a_theta / math.sqrt(d_model)).astype(jnp.bfloat16)
    b_piece = (b_theta / math.sqrt(R)).astype(jnp.bfloat16)
    a_factor = lax.all_gather(a_piece, "seq", axis=0, tiled=True)
    b_factor = lax.all_gather(b_piece, "seq", axis=0, tiled=True)
    proj = jnp.dot(tokens, a_factor, preferred_element_type=jnp.float32).astype(jnp.bfloat16)
    gate_full = lax.all_gather(gate_weight, "seq", axis=0, tiled=True)
    up_full = lax.all_gather(up_weight, "seq", axis=0, tiled=True)
    gate_base = jnp.dot(tokens, gate_full, preferred_element_type=jnp.float32)
    up_base = jnp.dot(tokens, up_full, preferred_element_type=jnp.float32)
    gate_pre = gate_base + jnp.dot(proj[:, :R], b_factor[:R], preferred_element_type=jnp.float32)
    up_pre = up_base + jnp.dot(proj[:, R:], b_factor[R:], preferred_element_type=jnp.float32)
    sig = jax.nn.sigmoid(gate_pre)
    act = gate_pre * sig
    hidden = (act * up_pre).astype(jnp.bfloat16)
    cot = cotangent.astype(jnp.float32)
    d_gate = (cot * up_pre * sig * (1.0 + gate_pre * (1.0 - sig))).astype(jnp.bfloat16)
    d_up = (cot * act).astype(jnp.bfloat16)
    rank_part = jnp.concatenate(
        [
            jnp.dot(d_gate, b_factor[:R].T, preferred_element_type=jnp.float32),
            jnp.dot(d_up, b_factor[R:].T, preferred_element_type=jnp.float32),
        ],
        axis=1,
    )
    back = jnp.dot(d_gate, gate_full.T, preferred_element_type=jnp.float32)
    back = back + jnp.dot(d_up, up_full.T, preferred_element_type=jnp.float32)
    term = back + jnp.dot(
        rank_part.astype(jnp.bfloat16), a_factor.T, preferred_element_type=jnp.float32
    )
    grad_tokens = lax.psum_scatter(
        term.astype(jnp.bfloat16), "tensor", scatter_dimension=0, tiled=True
    )
    b_part = jnp.concatenate(
        [contract_rows(proj[:, :R], d_gate), contract_rows(proj[:, R:], d_up)], axis=0
    ) / math.sqrt(tokens_all * R)
    rank_high = rank_part.astype(jnp.bfloat16)
    rank_low = (rank_part - rank_high.astype(jnp.float32)).astype(jnp.bfloat16)
    a_part = (contract_rows(tokens, rank_high) + contract_rows(tokens, rank_low)) / math.sqrt(
        tokens_all * d_model
    )
    a_seq = lax.psum_scatter(
        a_part.astype(jnp.bfloat16), "seq", scatter_dimension=0, tiled=True
    ).astype(jnp.float32)
    b_grad = lax.psum_scatter(
        b_part.astype(jnp.bfloat16), "seq", scatter_dimension=0, tiled=True
    ).astype(jnp.float32)
    a_grad = lax.psum(a_seq.astype(jnp.bfloat16), "tensor").astype(jnp.float32)
    a_new = ivon_update(a_mean, a_hess, a_moment, a_noise, scale_a, a_grad)
    b_new = ivon_update(b_mean, b_hess, b_moment, b_noise, scale_b, b_grad)
    return (hidden, grad_tokens, *a_new, *b_new)


def split_rank(value):
    row = lax.broadcasted_iota(jnp.int32, value.shape, 0)
    zero = jnp.zeros_like(value)
    return jnp.concatenate(
        [jnp.where(row < R, value, zero), jnp.where(row >= R, value, zero)], axis=1
    )


def fwd_kernel(zs, cnt, chunk, s_ref, tok_ref, a_ref, b_ref, *refs):
    cot_refs, refs = refs[:zs], refs[zs:]
    w_refs, refs = refs[: 2 * zs], refs[2 * zs :]
    hid_refs, refs = refs[:zs], refs[zs:]
    dg_ref, du_ref, bmat_ref, proj_ref, wcat_s, cot_s, hid_s = refs
    n = pl.program_id(0)
    z, core, col0 = s_ref[0], s_ref[1], s_ref[2]
    tiles = pl.num_programs(0)
    half = tok_ref.shape[3] // 2
    part = b_ref.shape[2]
    step = chunk // cnt
    m_all = tok_ref.shape[1] * cnt
    rows = m_all // zs

    def tok(q, step_at, lanes):
        at = pl.ds(step_at * step, step)
        return tok_ref[q, at, :, lanes].reshape(chunk, -1)

    def rows_at(step_at):
        return pl.ds(pl.multiple_of(step_at * chunk, 16), chunk)

    @pl.when(n == 0)
    def _():
        @pl.loop(0, m_all // chunk)
        def _(m):
            p = jnp.zeros((chunk, 2 * R), jnp.float32)
            for q in range(zs):
                for c in range(2):
                    p += jnp.dot(
                        tok(q, m, slice(c * half, (c + 1) * half)),
                        a_ref[jnp.bitwise_xor(core, c), jnp.bitwise_xor(z, q)],
                        preferred_element_type=jnp.float32,
                    )
            proj_ref[rows_at(m), :] = p.astype(jnp.bfloat16)

    for k in range(zs):
        q = jnp.bitwise_xor(z, k)
        for side in range(2):
            c = jnp.bitwise_xor(core, side)
            at = pl.ds(pl.multiple_of(c * half, LANE), half)
            w = w_refs[side * zs + k]
            wcat_s[q, at, :LANE] = w[0]
            wcat_s[q, at, LANE:] = w[1]
            at = pl.ds(pl.multiple_of((2 * q + c) * part, part), part)
            bmat_ref[at, :] = b_ref[side, k]
        cot_s[pl.ds(pl.multiple_of(q * rows, 16), rows), :] = cot_refs[k][...]
    keep = col0 + n >= z * tiles
    bb = split_rank(bmat_ref[...])

    @pl.loop(0, m_all // chunk)
    def _(m):
        at = rows_at(m)
        acc = jnp.dot(proj_ref[at, :], bb, preferred_element_type=jnp.float32)
        for q in range(zs):
            acc += jnp.dot(tok(q, m, slice(None)), wcat_s[q], preferred_element_type=jnp.float32)
        g, u = acc[:, :LANE], acc[:, LANE:]
        sig = jax.nn.sigmoid(g)
        act = g * sig
        hid_s[at, :] = (act * u).astype(jnp.bfloat16)
        cot = cot_s[at, :].astype(jnp.float32)
        dg = cot * u * sig * (1.0 + g * (1.0 - sig))
        dg_ref[at, :] = jnp.where(keep, dg, 0.0).astype(jnp.bfloat16)
        du_ref[at, :] = jnp.where(keep, cot * act, 0.0).astype(jnp.bfloat16)

    for k in range(zs):
        q = jnp.bitwise_xor(z, k)
        hid_refs[k][...] = hid_s[pl.ds(pl.multiple_of(q * rows, 16), rows), :]


def bwd_kernel(zs, ts, cnt, s_ref, dg_ref, du_ref, bmat_ref, a_ref, *refs):
    w_refs, refs = refs[: 2 * zs], refs[2 * zs :]
    outs, (rank_ref, d_s, rank_s) = refs[:4], refs[4:]
    i = pl.program_id(0)
    z, core, tensor = s_ref[0], s_ref[1], s_ref[3]
    wide = dg_ref.shape[1]

    def rows_of(s, k):
        m = (jnp.bitwise_xor(z, k) * ts + jnp.bitwise_xor(tensor, s)) * cnt
        return pl.ds(pl.multiple_of(m, 16), cnt)

    @pl.when(i == 0)
    def _():
        for s in range(ts):
            for k in range(zs):
                m = (s * zs + k) * cnt
                d_s[m : m + cnt, :wide] = dg_ref[rows_of(s, k), :]
                d_s[m : m + cnt, wide : 2 * wide] = du_ref[rows_of(s, k), :]
        rank_s[...] = contract_lanes(d_s[:, : 2 * wide], split_rank(bmat_ref[...]))
        d_s[:, 2 * wide :] = rank_s[...].astype(jnp.bfloat16)
        for s in range(ts):
            for k in range(zs):
                m = (s * zs + k) * cnt
                rank_ref[rows_of(s, k), :] = rank_s[m : m + cnt, :]

    for k in range(zs):
        q = jnp.bitwise_xor(z, k)
        w = []
        for side in range(2):
            ref = w_refs[side * zs + k]
            w.append(jnp.concatenate([ref[0], ref[1], a_ref[side, k]], axis=1))
        w = jnp.concatenate(w, axis=0)
        acc = contract_lanes(d_s[...], w).astype(jnp.bfloat16)
        for side in range(2):
            blk = 2 * q + jnp.bitwise_xor(core, side)
            part = acc[:, side * LANE : (side + 1) * LANE]
            for s in range(ts):
                for j in range(zs):
                    m = (s * zs + j) * cnt
                    low, first = j < zs // 2, (s & 1, s >> 1)
                    give = first[0] if low else first[1]
                    slot = first[1] if low else first[0]
                    out = outs[2 * (not low) + give]
                    out[slot, j % (zs // 2), blk] = part[m : m + cnt, :]


def place_kernel(zs, ts, own, sizes, wide, limit, s_ref, *refs):
    out_ref = refs[-1]
    for k in range(zs):
        at = jnp.minimum(jnp.bitwise_xor(s_ref[0], k) * wide, limit)
        at = pl.ds(pl.multiple_of(at, LANE), wide)
        for j, (off, cnt) in enumerate(sizes):
            for t in range(ts):
                out_ref[t * own + off : t * own + off + cnt, at] = refs[j * zs + k][
                    t * cnt : (t + 1) * cnt, :
                ]


def whole(shape):
    return pl.BlockSpec(shape, lambda i, s: (0,) * len(shape), pipeline_mode=pl.Buffered(1))


def forward(scalars, tok, a_all, b_all, cots, weights, off, cnt):
    zs, groups, _, quarter = tok.shape
    m_all = groups * cnt
    rows, wide = cots[0].shape
    half = weights[0].shape[1]
    chunk = m_all // max(1, m_all // 256)
    while chunk % cnt or m_all % chunk:
        chunk += 16
    bf = jnp.bfloat16
    return pl.pallas_call(
        functools.partial(fwd_kernel, zs, cnt, chunk),
        grid_spec=pltpu.PrefetchScalarGridSpec(
            num_scalar_prefetch=1,
            grid=(wide // LANE,),
            in_specs=[
                pl.BlockSpec(
                    (zs, groups, cnt, quarter),
                    lambda i, s: (0, 0, off // cnt, 0),
                    pipeline_mode=pl.Buffered(1),
                ),
                whole(a_all.shape),
                pl.BlockSpec((*b_all.shape[:3], LANE), lambda i, s: (0, 0, 0, i)),
            ]
            + [pl.BlockSpec((rows, LANE), lambda i, s: (0, i))] * zs
            + [pl.BlockSpec((2, half, LANE), lambda i, s: (0, 0, i))] * (2 * zs),
            out_specs=[pl.BlockSpec((rows, LANE), lambda i, s: (0, i))] * zs
            + [pl.BlockSpec((m_all, LANE), lambda i, s: (0, i))] * 2
            + [pl.BlockSpec((2 * R, LANE), lambda i, s: (0, i))]
            + [pl.BlockSpec((m_all, 2 * R), lambda i, s: (0, 0))],
            scratch_shapes=[
                pltpu.VMEM((zs, 2 * half, 2 * LANE), bf),
                pltpu.VMEM((m_all, LANE), bf),
                pltpu.VMEM((m_all, LANE), bf),
            ],
        ),
        out_shape=[jax.ShapeDtypeStruct((rows, wide), bf)] * zs
        + [jax.ShapeDtypeStruct((m_all, wide), bf)] * 2
        + [jax.ShapeDtypeStruct((2 * R, wide), bf)]
        + [jax.ShapeDtypeStruct((m_all, 2 * R), bf)],
        compiler_params=pltpu.CompilerParams(vmem_limit_bytes=44 << 20),
        cost_estimate=pl.CostEstimate(
            flops=2 * m_all * 2 * wide * (2 * zs * half),
            bytes_accessed=4 * zs * half * wide * 2 + m_all * (zs * quarter + 4 * wide) * 2,
            transcendentals=m_all * wide,
        ),
        name="fwd_columns",
    )(scalars, tok, a_all, b_all, *cots, *weights)


def backward(scalars, d_gate, d_up, bmat, a_all, weights, ts, cnt):
    zs = len(weights) // 2
    m_all, wide = d_gate.shape
    half = weights[0].shape[1]
    bf = jnp.bfloat16
    quarter = (ts // 2, zs // 2, 2 * zs, cnt)
    return pl.pallas_call(
        functools.partial(bwd_kernel, zs, ts, cnt),
        grid_spec=pltpu.PrefetchScalarGridSpec(
            num_scalar_prefetch=1,
            grid=(half // LANE,),
            in_specs=[whole(d_gate.shape), whole(d_up.shape), whole(bmat.shape)]
            + [pl.BlockSpec((2, zs, LANE, 2 * R), lambda i, s: (0, 0, i, 0))]
            + [pl.BlockSpec((2, LANE, wide), lambda i, s: (0, i, 0))] * (2 * zs),
            out_specs=[pl.BlockSpec((*quarter, LANE), lambda i, s: (0, 0, 0, 0, i))] * 4
            + [pl.BlockSpec((m_all, 2 * R), lambda i, s: (0, 0))],
            scratch_shapes=[
                pltpu.VMEM((m_all, 2 * wide + 2 * R), bf),
                pltpu.VMEM((m_all, 2 * R), jnp.float32),
            ],
        ),
        out_shape=[jax.ShapeDtypeStruct((*quarter, half), bf)] * 4
        + [jax.ShapeDtypeStruct((m_all, 2 * R), jnp.float32)],
        compiler_params=pltpu.CompilerParams(vmem_limit_bytes=44 << 20),
        cost_estimate=pl.CostEstimate(
            flops=2 * m_all * 2 * wide * (2 * zs * half),
            bytes_accessed=4 * zs * half * wide * 2 + m_all * (2 * zs * half + 2 * wide) * 2,
            transcendentals=0,
        ),
        name="bwd_columns",
    )(scalars, d_gate, d_up, bmat, a_all, *weights)


def pack(scalars, gate_weight, up_weight, k, wide, limit):
    half = gate_weight.shape[0]

    def tile(i, s):
        return (0, jnp.minimum(jnp.bitwise_xor(s[0], k) * wide, limit) // LANE + i)

    def kernel(s_ref, gate_ref, up_ref, out_ref):
        out_ref[0] = gate_ref[...]
        out_ref[1] = up_ref[...]

    return pl.pallas_call(
        kernel,
        grid_spec=pltpu.PrefetchScalarGridSpec(
            num_scalar_prefetch=1,
            grid=(wide // LANE,),
            in_specs=[pl.BlockSpec((half, LANE), tile)] * 2,
            out_specs=pl.BlockSpec((2, half, LANE), lambda i, s: (0, 0, i)),
        ),
        out_shape=jax.ShapeDtypeStruct((2, half, wide), jnp.bfloat16),
        compiler_params=pltpu.CompilerParams(vmem_limit_bytes=56 << 20),
        cost_estimate=pl.CostEstimate(
            flops=0, bytes_accessed=8 * half * wide, transcendentals=0
        ),
        name="pack_columns",
    )(scalars, gate_weight, up_weight)


def place(scalars, pieces, zs, ts, own, sizes, cols):
    wide = pieces[0].shape[1]
    return pl.pallas_call(
        functools.partial(place_kernel, zs, ts, own, sizes, wide, cols - wide),
        grid_spec=pltpu.PrefetchScalarGridSpec(
            num_scalar_prefetch=1,
            grid=(1,),
            in_specs=[whole(piece.shape) for piece in pieces],
            out_specs=whole((ts * own, cols)),
        ),
        out_shape=jax.ShapeDtypeStruct((ts * own, cols), jnp.bfloat16),
        compiler_params=pltpu.CompilerParams(vmem_limit_bytes=16 << 20),
        cost_estimate=pl.CostEstimate(
            flops=0, bytes_accessed=4 * ts * own * cols, transcendentals=0
        ),
        name="place_hidden",
    )(scalars, *pieces)


def after(value, *earlier):
    return lax.optimization_barrier((value, *earlier))[0]


def chunk_sizes(own):
    sizes, off = [], 0
    size = max(16, own * 2 // 5 // 16 * 16)
    while off < own:
        cnt = min(size, own - off)
        while off % cnt:
            cnt -= 16
        sizes.append((off, cnt))
        off += cnt
    return tuple(sizes)


def split_plan(
    tokens,
    gate_weight,
    up_weight,
    cotangent,
    a_mean,
    a_hess,
    a_moment,
    a_noise,
    b_mean,
    b_hess,
    b_moment,
    b_noise,
):
    seq_count = lax.axis_size("seq")
    ts = lax.axis_size("tensor")
    zs = seq_count // 2
    half, cols = gate_weight.shape
    d_model = half * seq_count
    rows = tokens.shape[0]
    tokens_all = rows * seq_count
    wide = -(-cols // (zs * LANE)) * LANE
    own = rows // ts
    part = 2 * R // seq_count
    seq = lax.axis_index("seq")
    z, core = seq // 2, seq % 2
    tensor = lax.axis_index("tensor")
    cores = [[2 * j + c for j in range(zs)] for c in range(2)]
    bf = jnp.bfloat16

    def start_of(chip):
        return jnp.minimum(chip * wide, cols - wide)

    def columns(value, k):
        at = start_of(jnp.bitwise_xor(z, k))
        return lax.dynamic_slice_in_dim(value, at, wide, value.ndim - 1)

    def over_z(value, k):
        if k == 0:
            return value
        return lax.ppermute(value, "seq", [(s, s ^ (2 * k)) for s in range(seq_count)])

    def over_core(value):
        return lax.ppermute(value, "seq", [(s, s ^ 1) for s in range(seq_count)])

    def over_tensor(value, k):
        return lax.ppermute(value, "tensor", [(t, t ^ k) for t in range(ts)])

    def wide_of(value):
        return value.astype(jnp.float32)

    scalars = jnp.stack([z, core, start_of(z) // LANE, tensor]).astype(jnp.int32)

    a_theta, scale_a = sample(a_mean, a_hess, a_noise)
    b_theta, scale_b = sample(b_mean, b_hess, b_noise)
    a_piece = (a_theta / math.sqrt(d_model)).astype(bf)
    b_piece = (b_theta / math.sqrt(R)).astype(bf)
    a_mine = jnp.stack([over_z(a_piece, k) for k in range(zs)])
    b_mine = jnp.stack([over_z(columns(b_piece, k), k) for k in range(zs)])
    a_all = jnp.stack([a_mine, over_core(a_mine)])
    b_all = jnp.stack([b_mine, over_core(b_mine)])

    pieces = [pack(scalars, gate_weight, up_weight, k, wide, cols - wide) for k in range(zs)]
    mine = [None] * zs
    mine[0] = pieces[0]
    for k in range(zs - 1, 0, -1):
        mine[k] = over_z(pieces[k], k)
    weights = mine + [over_core(piece) for piece in mine]

    sizes = chunk_sizes(own)
    quarter = d_model // ts
    tok = lax.dynamic_slice_in_dim(tokens, tensor * quarter, quarter, 1)
    tok = lax.all_gather(tok, "seq", axis=0, axis_index_groups=cores, tiled=True)
    tok = lax.all_gather(tok, "tensor", axis=0, tiled=False)

    def cotangent_of(j, *earlier):
        off, cnt = sizes[j]
        cot = cotangent.reshape(ts, own, cols)[:, off : off + cnt].reshape(ts * cnt, cols)
        cot = [columns(cot, k) for k in range(zs)]
        cot[1:] = [over_z(after(cot[k], *earlier), k) for k in range(1, zs)]
        return cot

    cot = cotangent_of(0)
    tok = tok.reshape(zs, zs * ts, own, quarter)

    hidden, grads, ranks = [], [], []
    d_all = []
    for j, (off, cnt) in enumerate(sizes):
        *hid, d_gate, d_up, bmat, proj = forward(scalars, tok, a_all, b_all, cot, weights, off, cnt)
        if j + 1 < len(sizes):
            cot = cotangent_of(j + 1, bmat)
        hidden += [over_z(hid[k], k) for k in range(zs)]
        x_keep, x_give, y_keep, y_give, rank = backward(
            scalars, d_gate, d_up, bmat, a_all, weights, ts, cnt
        )
        ranks.append(rank.reshape(zs * ts, cnt, 2 * R))
        d_all.append((proj, d_gate, d_up))
        x_got, y_got = over_tensor(x_give, 1), over_tensor(y_give, 2)
        x_next = (wide_of(x_keep[1]) + wide_of(x_got[1])).astype(bf)
        y_next = (wide_of(y_keep[1]) + wide_of(y_got[1])).astype(bf)
        x_last, y_last = over_tensor(x_next, 2), over_tensor(y_next, 1)
        parts = []
        for keep, got, last in ((x_keep, x_got, x_last), (y_keep, y_got, y_last)):
            for k in range(zs // 2):
                parts.append(wide_of(keep[0, k]) + wide_of(got[0, k]) + wide_of(last[k]))
        near = [over_z(parts[k].astype(bf), 1) for k in range(1, zs, 2)]
        parts = [parts[k] + wide_of(near[k // 2]) for k in range(0, zs, 2)]
        total = parts[0] + wide_of(over_z(parts[1].astype(bf), 2))
        grads.append(total.astype(bf))

    hidden = place(scalars, hidden, zs, ts, own, sizes, cols)
    grad_tokens = jnp.concatenate(grads, axis=1).transpose(1, 0, 2).reshape(own, d_model)

    rank = jnp.concatenate(ranks, axis=1).reshape(-1, 2 * R)
    rank_high = rank.astype(bf)
    rank_low = (rank - rank_high.astype(jnp.float32)).astype(bf)
    both = jnp.concatenate([rank_high, rank_low], axis=1)
    a_part = jnp.einsum(
        "qmd,mr->qdr",
        tok.reshape(zs, zs * rows, quarter),
        both,
        preferred_element_type=jnp.float32,
    )
    a_part = (a_part[..., : 2 * R] + a_part[..., 2 * R :]) / math.sqrt(tokens_all * d_model)
    a_part = a_part.reshape(zs, 2, half, 2 * R)
    a_keep = lax.dynamic_index_in_dim(a_part, core, 1, keepdims=False)
    a_give = lax.dynamic_index_in_dim(a_part, 1 - core, 1, keepdims=False)
    a_part = (a_keep + over_core(a_give.astype(bf)).astype(jnp.float32)).astype(bf)
    a_seq = jnp.zeros((half, 2 * R), jnp.float32)
    for k in range(zs):
        piece = lax.dynamic_index_in_dim(a_part, jnp.bitwise_xor(z, k), 0, keepdims=False)
        a_seq = a_seq + over_z(piece, k).astype(jnp.float32)
    a_seq = a_seq.astype(bf)
    a_grad = a_seq.astype(jnp.float32)
    for k in range(1, ts):
        a_grad = a_grad + wide_of(over_tensor(a_seq, k))

    b_part = jnp.zeros((2 * R, wide), jnp.float32)
    for left, d_gate, d_up in d_all:
        b_part = b_part + jnp.concatenate(
            [contract_rows(left[:, :R], d_gate), contract_rows(left[:, R:], d_up)], axis=0
        )
    b_part = (b_part / math.sqrt(tokens_all * R)).astype(bf)
    b_parts = lax.all_to_all(
        b_part.reshape(seq_count, part, wide), "seq", 0, 0, tiled=True
    ).astype(jnp.float32)
    b_parts = b_parts.reshape(zs, 2, part, wide).sum(1)
    b_grad = jnp.concatenate(
        [b_parts[j] for j in range(zs - 1)]
        + [b_parts[zs - 1][:, wide - (cols - (zs - 1) * wide) :]],
        axis=1,
    )

    a_new = ivon_update(a_mean, a_hess, a_moment, a_noise, scale_a, a_grad)
    b_new = ivon_update(b_mean, b_hess, b_moment, b_noise, scale_b, b_grad)
    return (hidden, grad_tokens, *a_new, *b_new)


def on_device(tokens, gate_weight, *rest):
    seq_count, ts = lax.axis_size("seq"), lax.axis_size("tensor")
    zs = seq_count // 2
    half, cols = gate_weight.shape
    rows = tokens.shape[0]
    wide = -(-cols // (zs * LANE)) * LANE
    fits = (
        seq_count == 2 * ts
        and ts == 4
        and half % LANE == 0
        and cols % LANE == 0
        and (zs - 1) * wide < cols
        and rows % (16 * ts) == 0
        and 2 * R == 16 * seq_count
        and rows * zs * half * seq_count * 2 <= 16 << 20
    )
    plan = split_plan if fits else gathered_plan
    return plan(tokens, gate_weight, *rest)


def solution(mesh):
    row, both = P("seq", None), P("seq", "tensor")
    in_specs = (row, both, both, both, row, row, row, row, both, both, both, both)
    out_specs = (both, P(("seq", "tensor"), None), row, row, row, both, both, both)
    return jax.shard_map(
        on_device, mesh=mesh, in_specs=in_specs, out_specs=out_specs, check_vma=False
    )
```

```python
import functools
import math

import jax
import jax.numpy as jnp
from jax import lax
from jax.experimental import pallas as pl
from jax.experimental.pallas import tpu as pltpu
from jax.sharding import PartitionSpec as P


R = 64
LANE = 128


ess = 8.0
decay = 0.001
beta_one = 0.9
beta_two = 0.99
rate = 0.1
debias = 1.0 - 0.9**10


def sample(mean, hess, noise):
    scale = jnp.sqrt(ess * (hess + decay))
    return (mean + noise / scale, scale)


def ivon_update(mean, hess, moment, noise, scale, grad):
    hess_hat = grad * noise * scale
    moment_new = beta_one * moment + (1.0 - beta_one) * grad
    diff = hess - hess_hat
    hess_new = (
        beta_two * hess
        + (1.0 - beta_two) * hess_hat
        + 0.5 * (1.0 - beta_two) ** 2 * diff * diff / (hess + decay)
    )
    mean_new = mean - rate * (moment_new / debias + decay * mean) / (hess_new + decay)
    return (mean_new, hess_new, moment_new)


def contract_rows(left, right):
    return lax.dot_general(
        left, right, (((0,), (0,)), ((), ())), preferred_element_type=jnp.float32
    )


def contract_lanes(left, right):
    return lax.dot_general(
        left, right, (((1,), (1,)), ((), ())), preferred_element_type=jnp.float32
    )


def gathered_plan(
    tokens,
    gate_weight,
    up_weight,
    cotangent,
    a_mean,
    a_hess,
    a_moment,
    a_noise,
    b_mean,
    b_hess,
    b_moment,
    b_noise,
):
    seq_count = lax.axis_size("seq")
    d_model = gate_weight.shape[0] * seq_count
    tokens_all = tokens.shape[0] * seq_count
    a_theta, scale_a = sample(a_mean, a_hess, a_noise)
    b_theta, scale_b = sample(b_mean, b_hess, b_noise)
    a_piece = (a_theta / math.sqrt(d_model)).astype(jnp.bfloat16)
    b_piece = (b_theta / math.sqrt(R)).astype(jnp.bfloat16)
    a_factor = lax.all_gather(a_piece, "seq", axis=0, tiled=True)
    b_factor = lax.all_gather(b_piece, "seq", axis=0, tiled=True)
    proj = jnp.dot(tokens, a_factor, preferred_element_type=jnp.float32).astype(jnp.bfloat16)
    gate_full = lax.all_gather(gate_weight, "seq", axis=0, tiled=True)
    up_full = lax.all_gather(up_weight, "seq", axis=0, tiled=True)
    gate_base = jnp.dot(tokens, gate_full, preferred_element_type=jnp.float32)
    up_base = jnp.dot(tokens, up_full, preferred_element_type=jnp.float32)
    gate_pre = gate_base + jnp.dot(proj[:, :R], b_factor[:R], preferred_element_type=jnp.float32)
    up_pre = up_base + jnp.dot(proj[:, R:], b_factor[R:], preferred_element_type=jnp.float32)
    sig = jax.nn.sigmoid(gate_pre)
    act = gate_pre * sig
    hidden = (act * up_pre).astype(jnp.bfloat16)
    cot = cotangent.astype(jnp.float32)
    d_gate = (cot * up_pre * sig * (1.0 + gate_pre * (1.0 - sig))).astype(jnp.bfloat16)
    d_up = (cot * act).astype(jnp.bfloat16)
    rank_part = jnp.concatenate(
        [
            jnp.dot(d_gate, b_factor[:R].T, preferred_element_type=jnp.float32),
            jnp.dot(d_up, b_factor[R:].T, preferred_element_type=jnp.float32),
        ],
        axis=1,
    )
    back = jnp.dot(d_gate, gate_full.T, preferred_element_type=jnp.float32)
    back = back + jnp.dot(d_up, up_full.T, preferred_element_type=jnp.float32)
    term = back + jnp.dot(
        rank_part.astype(jnp.bfloat16), a_factor.T, preferred_element_type=jnp.float32
    )
    grad_tokens = lax.psum_scatter(
        term.astype(jnp.bfloat16), "tensor", scatter_dimension=0, tiled=True
    )
    b_part = jnp.concatenate(
        [contract_rows(proj[:, :R], d_gate), contract_rows(proj[:, R:], d_up)], axis=0
    ) / math.sqrt(tokens_all * R)
    rank_high = rank_part.astype(jnp.bfloat16)
    rank_low = (rank_part - rank_high.astype(jnp.float32)).astype(jnp.bfloat16)
    a_part = (contract_rows(tokens, rank_high) + contract_rows(tokens, rank_low)) / math.sqrt(
        tokens_all * d_model
    )
    a_seq = lax.psum_scatter(
        a_part.astype(jnp.bfloat16), "seq", scatter_dimension=0, tiled=True
    ).astype(jnp.float32)
    b_grad = lax.psum_scatter(
        b_part.astype(jnp.bfloat16), "seq", scatter_dimension=0, tiled=True
    ).astype(jnp.float32)
    a_grad = lax.psum(a_seq.astype(jnp.bfloat16), "tensor").astype(jnp.float32)
    a_new = ivon_update(a_mean, a_hess, a_moment, a_noise, scale_a, a_grad)
    b_new = ivon_update(b_mean, b_hess, b_moment, b_noise, scale_b, b_grad)
    return (hidden, grad_tokens, *a_new, *b_new)


def split_rank(value):
    row = lax.broadcasted_iota(jnp.int32, value.shape, 0)
    zero = jnp.zeros_like(value)
    return jnp.concatenate(
        [jnp.where(row < R, value, zero), jnp.where(row >= R, value, zero)], axis=1
    )


def fwd_kernel(zs, cnt, chunk, s_ref, tok_ref, a_ref, b_ref, *refs):
    cot_refs, refs = refs[:zs], refs[zs:]
    w_refs, refs = refs[: 2 * zs], refs[2 * zs :]
    hid_refs, refs = refs[:zs], refs[zs:]
    dg_ref, du_ref, bmat_ref, proj_ref, wcat_s, cot_s, hid_s = refs
    n = pl.program_id(0)
    z, core, col0 = s_ref[0], s_ref[1], s_ref[2]
    tiles = pl.num_programs(0)
    half = tok_ref.shape[3] // 2
    part = b_ref.shape[2]
    step = chunk // cnt
    m_all = tok_ref.shape[1] * cnt
    rows = m_all // zs

    def tok(q, step_at, lanes):
        at = pl.ds(step_at * step, step)
        return tok_ref[q, at, :, lanes].reshape(chunk, -1)

    def rows_at(step_at):
        return pl.ds(pl.multiple_of(step_at * chunk, 16), chunk)

    @pl.when(n == 0)
    def _():
        @pl.loop(0, m_all // chunk)
        def _(m):
            p = jnp.zeros((chunk, 2 * R), jnp.float32)
            for q in range(zs):
                for c in range(2):
                    p += jnp.dot(
                        tok(q, m, slice(c * half, (c + 1) * half)),
                        a_ref[jnp.bitwise_xor(core, c), jnp.bitwise_xor(z, q)],
                        preferred_element_type=jnp.float32,
                    )
            proj_ref[rows_at(m), :] = p.astype(jnp.bfloat16)

    for k in range(zs):
        q = jnp.bitwise_xor(z, k)
        for side in range(2):
            c = jnp.bitwise_xor(core, side)
            at = pl.ds(pl.multiple_of(c * half, LANE), half)
            w = w_refs[side * zs + k]
            wcat_s[q, at, :LANE] = w[0]
            wcat_s[q, at, LANE:] = w[1]
            at = pl.ds(pl.multiple_of((2 * q + c) * part, part), part)
            bmat_ref[at, :] = b_ref[side, k]
        cot_s[pl.ds(pl.multiple_of(q * rows, 16), rows), :] = cot_refs[k][...]
    keep = col0 + n >= z * tiles
    bb = split_rank(bmat_ref[...])

    for m in range(m_all // chunk):
        at = slice(m * chunk, (m + 1) * chunk)
        acc = jnp.dot(proj_ref[at, :], bb, preferred_element_type=jnp.float32)
        for q in range(zs):
            acc += jnp.dot(tok(q, m, slice(None)), wcat_s[q], preferred_element_type=jnp.float32)
        g, u = acc[:, :LANE], acc[:, LANE:]
        sig = jax.nn.sigmoid(g)
        act = g * sig
        hid_s[at, :] = (act * u).astype(jnp.bfloat16)
        cot = cot_s[at, :].astype(jnp.float32)
        dg = cot * u * sig * (1.0 + g * (1.0 - sig))
        dg_ref[at, :] = jnp.where(keep, dg, 0.0).astype(jnp.bfloat16)
        du_ref[at, :] = jnp.where(keep, cot * act, 0.0).astype(jnp.bfloat16)

    for k in range(zs):
        q = jnp.bitwise_xor(z, k)
        hid_refs[k][...] = hid_s[pl.ds(pl.multiple_of(q * rows, 16), rows), :]


def bwd_kernel(zs, ts, cnt, s_ref, dg_ref, du_ref, bmat_ref, a_ref, *refs):
    w_refs, refs = refs[: 2 * zs], refs[2 * zs :]
    outs, (rank_ref, d_s, rank_s) = refs[:4], refs[4:]
    i = pl.program_id(0)
    z, core, tensor = s_ref[0], s_ref[1], s_ref[3]
    wide = dg_ref.shape[1]

    def rows_of(s, k):
        m = (jnp.bitwise_xor(z, k) * ts + jnp.bitwise_xor(tensor, s)) * cnt
        return pl.ds(pl.multiple_of(m, 16), cnt)

    @pl.when(i == 0)
    def _():
        for s in range(ts):
            for k in range(zs):
                m = (s * zs + k) * cnt
                d_s[m : m + cnt, :wide] = dg_ref[rows_of(s, k), :]
                d_s[m : m + cnt, wide : 2 * wide] = du_ref[rows_of(s, k), :]
        rank_s[...] = contract_lanes(d_s[:, : 2 * wide], split_rank(bmat_ref[...]))
        d_s[:, 2 * wide :] = rank_s[...].astype(jnp.bfloat16)
        for s in range(ts):
            for k in range(zs):
                m = (s * zs + k) * cnt
                rank_ref[rows_of(s, k), :] = rank_s[m : m + cnt, :]

    for k in range(zs):
        q = jnp.bitwise_xor(z, k)
        w = []
        for side in range(2):
            ref = w_refs[side * zs + k]
            w.append(jnp.concatenate([ref[0], ref[1], a_ref[side, k]], axis=1))
        w = jnp.concatenate(w, axis=0)
        acc = contract_lanes(d_s[...], w).astype(jnp.bfloat16)
        for side in range(2):
            blk = 2 * q + jnp.bitwise_xor(core, side)
            part = acc[:, side * LANE : (side + 1) * LANE]
            for s in range(ts):
                for j in range(zs):
                    m = (s * zs + j) * cnt
                    low, first = j < zs // 2, (s & 1, s >> 1)
                    give = first[0] if low else first[1]
                    slot = first[1] if low else first[0]
                    out = outs[2 * (not low) + give]
                    out[slot, j % (zs // 2), blk] = part[m : m + cnt, :]


def place_kernel(zs, ts, own, sizes, wide, limit, s_ref, *refs):
    out_ref = refs[-1]
    for k in range(zs):
        at = jnp.minimum(jnp.bitwise_xor(s_ref[0], k) * wide, limit)
        at = pl.ds(pl.multiple_of(at, LANE), wide)
        for j, (off, cnt) in enumerate(sizes):
            for t in range(ts):
                out_ref[t * own + off : t * own + off + cnt, at] = refs[j * zs + k][
                    t * cnt : (t + 1) * cnt, :
                ]


def whole(shape):
    return pl.BlockSpec(shape, lambda i, s: (0,) * len(shape), pipeline_mode=pl.Buffered(1))


def forward(scalars, tok, a_all, b_all, cots, weights, off, cnt):
    zs, groups, _, quarter = tok.shape
    m_all = groups * cnt
    rows, wide = cots[0].shape
    half = weights[0].shape[1]
    chunk = m_all // max(1, m_all // 256)
    while chunk % cnt or m_all % chunk:
        chunk += 16
    bf = jnp.bfloat16
    return pl.pallas_call(
        functools.partial(fwd_kernel, zs, cnt, chunk),
        grid_spec=pltpu.PrefetchScalarGridSpec(
            num_scalar_prefetch=1,
            grid=(wide // LANE,),
            in_specs=[
                pl.BlockSpec(
                    (zs, groups, cnt, quarter),
                    lambda i, s: (0, 0, off // cnt, 0),
                    pipeline_mode=pl.Buffered(1),
                ),
                whole(a_all.shape),
                pl.BlockSpec((*b_all.shape[:3], LANE), lambda i, s: (0, 0, 0, i)),
            ]
            + [pl.BlockSpec((rows, LANE), lambda i, s: (0, i))] * zs
            + [pl.BlockSpec((2, half, LANE), lambda i, s: (0, 0, i))] * (2 * zs),
            out_specs=[pl.BlockSpec((rows, LANE), lambda i, s: (0, i))] * zs
            + [pl.BlockSpec((m_all, LANE), lambda i, s: (0, i))] * 2
            + [pl.BlockSpec((2 * R, LANE), lambda i, s: (0, i))]
            + [pl.BlockSpec((m_all, 2 * R), lambda i, s: (0, 0))],
            scratch_shapes=[
                pltpu.VMEM((zs, 2 * half, 2 * LANE), bf),
                pltpu.VMEM((m_all, LANE), bf),
                pltpu.VMEM((m_all, LANE), bf),
            ],
        ),
        out_shape=[jax.ShapeDtypeStruct((rows, wide), bf)] * zs
        + [jax.ShapeDtypeStruct((m_all, wide), bf)] * 2
        + [jax.ShapeDtypeStruct((2 * R, wide), bf)]
        + [jax.ShapeDtypeStruct((m_all, 2 * R), bf)],
        compiler_params=pltpu.CompilerParams(vmem_limit_bytes=44 << 20),
        cost_estimate=pl.CostEstimate(
            flops=2 * m_all * 2 * wide * (2 * zs * half),
            bytes_accessed=4 * zs * half * wide * 2 + m_all * (zs * quarter + 4 * wide) * 2,
            transcendentals=m_all * wide,
        ),
        name="fwd_columns",
    )(scalars, tok, a_all, b_all, *cots, *weights)


def backward(scalars, d_gate, d_up, bmat, a_all, weights, ts, cnt):
    zs = len(weights) // 2
    m_all, wide = d_gate.shape
    half = weights[0].shape[1]
    bf = jnp.bfloat16
    quarter = (ts // 2, zs // 2, 2 * zs, cnt)
    return pl.pallas_call(
        functools.partial(bwd_kernel, zs, ts, cnt),
        grid_spec=pltpu.PrefetchScalarGridSpec(
            num_scalar_prefetch=1,
            grid=(half // LANE,),
            in_specs=[whole(d_gate.shape), whole(d_up.shape), whole(bmat.shape)]
            + [pl.BlockSpec((2, zs, LANE, 2 * R), lambda i, s: (0, 0, i, 0))]
            + [pl.BlockSpec((2, LANE, wide), lambda i, s: (0, i, 0))] * (2 * zs),
            out_specs=[pl.BlockSpec((*quarter, LANE), lambda i, s: (0, 0, 0, 0, i))] * 4
            + [pl.BlockSpec((m_all, 2 * R), lambda i, s: (0, 0))],
            scratch_shapes=[
                pltpu.VMEM((m_all, 2 * wide + 2 * R), bf),
                pltpu.VMEM((m_all, 2 * R), jnp.float32),
            ],
        ),
        out_shape=[jax.ShapeDtypeStruct((*quarter, half), bf)] * 4
        + [jax.ShapeDtypeStruct((m_all, 2 * R), jnp.float32)],
        compiler_params=pltpu.CompilerParams(vmem_limit_bytes=44 << 20),
        cost_estimate=pl.CostEstimate(
            flops=2 * m_all * 2 * wide * (2 * zs * half),
            bytes_accessed=4 * zs * half * wide * 2 + m_all * (2 * zs * half + 2 * wide) * 2,
            transcendentals=0,
        ),
        name="bwd_columns",
    )(scalars, d_gate, d_up, bmat, a_all, *weights)


def pack(scalars, gate_weight, up_weight, k, wide, limit):
    half = gate_weight.shape[0]

    def tile(i, s):
        return (0, jnp.minimum(jnp.bitwise_xor(s[0], k) * wide, limit) // LANE + i)

    def kernel(s_ref, gate_ref, up_ref, out_ref):
        out_ref[0] = gate_ref[...]
        out_ref[1] = up_ref[...]

    return pl.pallas_call(
        kernel,
        grid_spec=pltpu.PrefetchScalarGridSpec(
            num_scalar_prefetch=1,
            grid=(wide // LANE,),
            in_specs=[pl.BlockSpec((half, LANE), tile)] * 2,
            out_specs=pl.BlockSpec((2, half, LANE), lambda i, s: (0, 0, i)),
        ),
        out_shape=jax.ShapeDtypeStruct((2, half, wide), jnp.bfloat16),
        compiler_params=pltpu.CompilerParams(vmem_limit_bytes=56 << 20),
        cost_estimate=pl.CostEstimate(
            flops=0, bytes_accessed=8 * half * wide, transcendentals=0
        ),
        name="pack_columns",
    )(scalars, gate_weight, up_weight)


def place(scalars, pieces, zs, ts, own, sizes, cols):
    wide = pieces[0].shape[1]
    return pl.pallas_call(
        functools.partial(place_kernel, zs, ts, own, sizes, wide, cols - wide),
        grid_spec=pltpu.PrefetchScalarGridSpec(
            num_scalar_prefetch=1,
            grid=(1,),
            in_specs=[whole(piece.shape) for piece in pieces],
            out_specs=whole((ts * own, cols)),
        ),
        out_shape=jax.ShapeDtypeStruct((ts * own, cols), jnp.bfloat16),
        compiler_params=pltpu.CompilerParams(vmem_limit_bytes=16 << 20),
        cost_estimate=pl.CostEstimate(
            flops=0, bytes_accessed=4 * ts * own * cols, transcendentals=0
        ),
        name="place_hidden",
    )(scalars, *pieces)


def after(value, *earlier):
    return lax.optimization_barrier((value, *earlier))[0]


def chunk_sizes(own):
    sizes, off = [], 0
    size = max(16, own * 2 // 5 // 16 * 16)
    while off < own:
        cnt = min(size, own - off)
        while off % cnt:
            cnt -= 16
        sizes.append((off, cnt))
        off += cnt
    return tuple(sizes)


def split_plan(
    tokens,
    gate_weight,
    up_weight,
    cotangent,
    a_mean,
    a_hess,
    a_moment,
    a_noise,
    b_mean,
    b_hess,
    b_moment,
    b_noise,
):
    seq_count = lax.axis_size("seq")
    ts = lax.axis_size("tensor")
    zs = seq_count // 2
    half, cols = gate_weight.shape
    d_model = half * seq_count
    rows = tokens.shape[0]
    tokens_all = rows * seq_count
    wide = -(-cols // (zs * LANE)) * LANE
    own = rows // ts
    part = 2 * R // seq_count
    seq = lax.axis_index("seq")
    z, core = seq // 2, seq % 2
    tensor = lax.axis_index("tensor")
    cores = [[2 * j + c for j in range(zs)] for c in range(2)]
    bf = jnp.bfloat16

    def start_of(chip):
        return jnp.minimum(chip * wide, cols - wide)

    def columns(value, k):
        at = start_of(jnp.bitwise_xor(z, k))
        return lax.dynamic_slice_in_dim(value, at, wide, value.ndim - 1)

    def over_z(value, k):
        if k == 0:
            return value
        return lax.ppermute(value, "seq", [(s, s ^ (2 * k)) for s in range(seq_count)])

    def over_core(value):
        return lax.ppermute(value, "seq", [(s, s ^ 1) for s in range(seq_count)])

    def over_tensor(value, k):
        return lax.ppermute(value, "tensor", [(t, t ^ k) for t in range(ts)])

    def wide_of(value):
        return value.astype(jnp.float32)

    scalars = jnp.stack([z, core, start_of(z) // LANE, tensor]).astype(jnp.int32)

    a_theta, scale_a = sample(a_mean, a_hess, a_noise)
    b_theta, scale_b = sample(b_mean, b_hess, b_noise)
    a_piece = (a_theta / math.sqrt(d_model)).astype(bf)
    b_piece = (b_theta / math.sqrt(R)).astype(bf)
    a_mine = jnp.stack([over_z(a_piece, k) for k in range(zs)])
    b_mine = jnp.stack([over_z(columns(b_piece, k), k) for k in range(zs)])
    a_all = jnp.stack([a_mine, over_core(a_mine)])
    b_all = jnp.stack([b_mine, over_core(b_mine)])

    pieces = [pack(scalars, gate_weight, up_weight, k, wide, cols - wide) for k in range(zs)]
    mine = [None] * zs
    mine[0] = pieces[0]
    for k in range(zs - 1, 0, -1):
        mine[k] = over_z(pieces[k], k)
    weights = mine + [over_core(piece) for piece in mine]

    sizes = chunk_sizes(own)
    quarter = d_model // ts
    tok = lax.dynamic_slice_in_dim(tokens, tensor * quarter, quarter, 1)
    tok = lax.all_gather(tok, "seq", axis=0, axis_index_groups=cores, tiled=True)
    tok = lax.all_gather(tok, "tensor", axis=0, tiled=False)

    def cotangent_of(j, *earlier):
        off, cnt = sizes[j]
        cot = cotangent.reshape(ts, own, cols)[:, off : off + cnt].reshape(ts * cnt, cols)
        cot = [columns(cot, k) for k in range(zs)]
        cot[1:] = [over_z(after(cot[k], *earlier), k) for k in range(1, zs)]
        return cot

    cot = cotangent_of(0)
    tok = tok.reshape(zs, zs * ts, own, quarter)

    hidden, grads, ranks = [], [], []
    d_all = []
    for j, (off, cnt) in enumerate(sizes):
        *hid, d_gate, d_up, bmat, proj = forward(scalars, tok, a_all, b_all, cot, weights, off, cnt)
        if j + 1 < len(sizes):
            cot = cotangent_of(j + 1, bmat)
        hidden += [over_z(hid[k], k) for k in range(zs)]
        x_keep, x_give, y_keep, y_give, rank = backward(
            scalars, d_gate, d_up, bmat, a_all, weights, ts, cnt
        )
        ranks.append(rank.reshape(zs * ts, cnt, 2 * R))
        d_all.append((proj, d_gate, d_up))
        x_got, y_got = over_tensor(x_give, 1), over_tensor(y_give, 2)
        x_next = (wide_of(x_keep[1]) + wide_of(x_got[1])).astype(bf)
        y_next = (wide_of(y_keep[1]) + wide_of(y_got[1])).astype(bf)
        x_last, y_last = over_tensor(x_next, 2), over_tensor(y_next, 1)
        parts = []
        for keep, got, last in ((x_keep, x_got, x_last), (y_keep, y_got, y_last)):
            for k in range(zs // 2):
                parts.append(wide_of(keep[0, k]) + wide_of(got[0, k]) + wide_of(last[k]))
        near = [over_z(parts[k].astype(bf), 1) for k in range(1, zs, 2)]
        parts = [parts[k] + wide_of(near[k // 2]) for k in range(0, zs, 2)]
        total = parts[0] + wide_of(over_z(parts[1].astype(bf), 2))
        grads.append(total.astype(bf))

    hidden = place(scalars, hidden, zs, ts, own, sizes, cols)
    grad_tokens = jnp.concatenate(grads, axis=1).transpose(1, 0, 2).reshape(own, d_model)

    rank = jnp.concatenate(ranks, axis=1).reshape(-1, 2 * R)
    rank_high = rank.astype(bf)
    rank_low = (rank - rank_high.astype(jnp.float32)).astype(bf)
    both = jnp.concatenate([rank_high, rank_low], axis=1)
    a_part = jnp.einsum(
        "qmd,mr->qdr",
        tok.reshape(zs, zs * rows, quarter),
        both,
        preferred_element_type=jnp.float32,
    )
    a_part = (a_part[..., : 2 * R] + a_part[..., 2 * R :]) / math.sqrt(tokens_all * d_model)
    a_part = a_part.reshape(zs, 2, half, 2 * R)
    a_keep = lax.dynamic_index_in_dim(a_part, core, 1, keepdims=False)
    a_give = lax.dynamic_index_in_dim(a_part, 1 - core, 1, keepdims=False)
    a_part = (a_keep + over_core(a_give.astype(bf)).astype(jnp.float32)).astype(bf)
    a_seq = jnp.zeros((half, 2 * R), jnp.float32)
    for k in range(zs):
        piece = lax.dynamic_index_in_dim(a_part, jnp.bitwise_xor(z, k), 0, keepdims=False)
        a_seq = a_seq + over_z(piece, k).astype(jnp.float32)
    a_seq = a_seq.astype(bf)
    a_grad = a_seq.astype(jnp.float32)
    for k in range(1, ts):
        a_grad = a_grad + wide_of(over_tensor(a_seq, k))

    b_part = jnp.zeros((2 * R, wide), jnp.float32)
    for left, d_gate, d_up in d_all:
        b_part = b_part + jnp.concatenate(
            [contract_rows(left[:, :R], d_gate), contract_rows(left[:, R:], d_up)], axis=0
        )
    b_part = (b_part / math.sqrt(tokens_all * R)).astype(bf)
    b_parts = lax.all_to_all(
        b_part.reshape(seq_count, part, wide), "seq", 0, 0, tiled=True
    ).astype(jnp.float32)
    b_parts = b_parts.reshape(zs, 2, part, wide).sum(1)
    b_grad = jnp.concatenate(
        [b_parts[j] for j in range(zs - 1)]
        + [b_parts[zs - 1][:, wide - (cols - (zs - 1) * wide) :]],
        axis=1,
    )

    a_new = ivon_update(a_mean, a_hess, a_moment, a_noise, scale_a, a_grad)
    b_new = ivon_update(b_mean, b_hess, b_moment, b_noise, scale_b, b_grad)
    return (hidden, grad_tokens, *a_new, *b_new)


def on_device(tokens, gate_weight, *rest):
    seq_count, ts = lax.axis_size("seq"), lax.axis_size("tensor")
    zs = seq_count // 2
    half, cols = gate_weight.shape
    rows = tokens.shape[0]
    wide = -(-cols // (zs * LANE)) * LANE
    fits = (
        seq_count == 2 * ts
        and ts == 4
        and half % LANE == 0
        and cols % LANE == 0
        and (zs - 1) * wide < cols
        and rows % (16 * ts) == 0
        and 2 * R == 16 * seq_count
        and rows * zs * half * seq_count * 2 <= 16 << 20
    )
    plan = split_plan if fits else gathered_plan
    return plan(tokens, gate_weight, *rest)


def solution(mesh):
    row, both = P("seq", None), P("seq", "tensor")
    in_specs = (row, both, both, both, row, row, row, row, both, both, both, both)
    out_specs = (both, P(("seq", "tensor"), None), row, row, row, both, both, both)
    return jax.shard_map(
        on_device, mesh=mesh, in_specs=in_specs, out_specs=out_specs, check_vma=False
    )
```
